32 devices in a mesh: fsdp: 4 (over y, core), tensor: 8 (over z, x).
Axes of the slice: x: 2, y: 2, z: 4, core: 2. Of those that a mesh axis runs over, the one named last changes fastest.
Arguments:
- activations: bfloat16 [4096, 8192], P('fsdp', 'tensor'), may hold values from -6 to 6
- first_factor: bfloat16 [64, 128, 512], P('tensor', 'fsdp'), may hold values from -0.5 to 0.5
- second_factor: bfloat16 [64, 512, 512], P('tensor', 'fsdp'), may hold values from -0.25 to 0.25
- third_factor: bfloat16 [64, 512, 512], P('tensor', 'fsdp'), may hold values from -0.25 to 0.25
- fourth_factor: bfloat16 [64, 512, 128], P('tensor', 'fsdp'), may hold values from -0.25 to 0.25
- out_grad: bfloat16 [4096, 8192], P('fsdp', 'tensor'), may hold values from -6 to 6
Outputs:
- result: bfloat16 [4096, 8192], P('fsdp', 'tensor')
- in_grad: bfloat16 [4096, 8192], P('fsdp', 'tensor')
- first_grad: float32 [64, 128, 512], P('tensor', 'fsdp')
- second_grad: float32 [64, 512, 512], P('tensor', 'fsdp')
- third_grad: float32 [64, 512, 512], P('tensor', 'fsdp')
- fourth_grad: float32 [64, 512, 128], P('tensor', 'fsdp')
The draws below stay inside these ranges and needn't reach their ends.
All inputs are finite; a program needn't handle non-finite values.
Results may differ from the reference program's by a relative error of at most 0.014.
Values may be sent and summed in bfloat16 or wider, within the bound.
A program may use at most 128 MiB of HBM per device.

```python
import jax
import jax.numpy as jnp
from jax import lax

D = 8192
NB = 64
DB = 128
HB = 512
K = 8
TOKENS = 4096


def block_scale(own_key, dims, pieces, least, top_value):
    loudness, own = 1.0, jax.random.fold_in(own_key, 6)
    for axis_at, blocks in pieces:
        heights = jnp.exp(jax.random.uniform(jax.random.fold_in(own, axis_at), (blocks,), jnp.float32, least / len(pieces), top_value / len(pieces)))
        loudness = loudness * jnp.repeat(heights, dims[axis_at] // blocks).reshape([-1 if axis == axis_at else 1 for axis in range(len(dims))])
    return loudness


def centred(key, shape, width, limit, pieces=(), kind=jnp.bfloat16):
    level = block_scale(key, shape, pieces, -0.22, 0.18) if pieces else 1.0
    drawn = jax.random.normal(key, shape, jnp.float32) * width * level
    return jnp.minimum(jnp.maximum(drawn, -limit), limit).astype(kind)


def setup_inputs(seed: int = 0) -> dict:
    arg_keys = jax.random.split(jax.random.key(seed), 7)
    return {
        "activations": centred(arg_keys[0], (TOKENS, D), 1.0, 6.0, ((0, 4), (1, 8))),
        "first_factor": centred(arg_keys[1], (NB, DB, HB), DB ** -0.5, 0.5, ((0, 8), (1, 4))),
        "second_factor": centred(arg_keys[2], (NB, HB, HB), HB ** -0.5, 0.25, ((0, 8), (1, 4))),
        "third_factor": centred(arg_keys[3], (NB, HB, HB), HB ** -0.5, 0.25, ((0, 8), (1, 4))),
        "fourth_factor": centred(arg_keys[4], (NB, HB, DB), HB ** -0.5, 0.25, ((0, 8), (1, 4))),
        "out_grad": centred(arg_keys[5], (TOKENS, D), 1.0, 6.0, ((0, 4), (1, 8))),
    }


def gelu_value(v):
    return 0.5 * v * (1.0 + lax.erf(v * 0.7071067811865476))


def gelu_slope(v):
    return 0.5 * (1.0 + lax.erf(v * 0.7071067811865476)) + v * jnp.exp(-0.5 * v * v) * 0.3989422804014327


def regroup(arr):
    total = arr.shape[0]
    return arr.reshape(total, NB, NB, K).transpose(0, 2, 1, 3).reshape(total, NB, HB)


def reference(activations, first_factor, second_factor, third_factor, fourth_factor, out_grad):
    f32 = jnp.float32
    total = activations.shape[0]
    inputs = activations.reshape(total, NB, DB).astype(f32)
    wone = first_factor.astype(f32)
    wtwo = second_factor.astype(f32)
    wthree = third_factor.astype(f32)
    wfour = fourth_factor.astype(f32)
    first_out = jnp.einsum('tbi,bij->tbj', inputs, wone).astype(jnp.bfloat16)
    mixed_in = regroup(first_out).astype(f32)
    pre = jnp.einsum('tcp,cpm->tcm', mixed_in, wtwo)
    hidden = gelu_value(pre).astype(jnp.bfloat16).astype(f32)
    down = jnp.einsum('tcm,cmn->tcn', hidden, wthree).astype(jnp.bfloat16)
    regrouped = regroup(down).astype(f32)
    result = jnp.einsum('tbp,bpo->tbo', regrouped, wfour).reshape(total, D).astype(jnp.bfloat16)
    grad_out = out_grad.reshape(total, NB, DB).astype(f32)
    fourth_grad = jnp.einsum('tbp,tbo->bpo', regrouped, grad_out)
    dw = jnp.einsum('tbo,bpo->tbp', grad_out, wfour).astype(jnp.bfloat16)
    ddown = regroup(dw).astype(f32)
    third_grad = jnp.einsum('tcm,tcn->cmn', hidden, ddown)
    dhidden = jnp.einsum('tcn,cmn->tcm', ddown, wthree)
    dpre = (dhidden * gelu_slope(pre)).astype(jnp.bfloat16).astype(f32)
    second_grad = jnp.einsum('tcp,tcm->cpm', mixed_in, dpre)
    dz = jnp.einsum('tcm,cpm->tcp', dpre, wtwo).astype(jnp.bfloat16)
    dy = regroup(dz).astype(f32)
    first_grad = jnp.einsum('tbi,tbj->bij', inputs, dy)
    in_grad = jnp.einsum('tbj,bij->tbi', dy, wone).reshape(total, D).astype(jnp.bfloat16)
    return (result, in_grad, first_grad, second_grad, third_grad, fourth_grad)
```

```python
import jax
import jax.numpy as jnp
from jax import lax
from jax.sharding import PartitionSpec as P

D = 8192
NB = 64
HB = 512
F32 = jnp.float32
BF16 = jnp.bfloat16


def gelu_both(v):
    half = 0.5 * (1.0 + lax.erf(v * 0.7071067811865476))
    slope = half + v * jnp.exp(-0.5 * v * v) * 0.3989422804014327
    return v * half, slope


def fetch(shard):
    return lax.all_gather(shard, "fsdp", axis=1, tiled=True)


def split_units(arr):
    blocks, units, tok = arr.shape
    return arr.reshape(blocks, NB, units // NB, tok).transpose(1, 0, 2, 3)


def send(parts):
    return lax.all_to_all(parts, "tensor", split_axis=0, concat_axis=0, tiled=True)


def join_halves(halves, groups):
    parts = [h.reshape(groups, -1, *h.shape[1:]) for h in halves]
    arr = parts[0] if len(parts) == 1 else jnp.concatenate(parts, axis=2)
    own, tok = arr.shape[1], arr.shape[4]
    return arr.transpose(1, 0, 2, 3, 4).reshape(own, HB, tok)


def follow(value, done):
    return lax.optimization_barrier((value, done))


def scatter(grad):
    return lax.psum_scatter(
        grad.astype(BF16), "fsdp", scatter_dimension=1, tiled=True
    ).astype(F32)


def local(activations, first_factor, second_factor, third_factor, fourth_factor, out_grad):
    tok = activations.shape[0]
    local_blocks = second_factor.shape[0]
    block_in = D // NB
    inputs = activations.reshape(tok, local_blocks, block_in)
    grad_out = out_grad.reshape(tok, local_blocks, block_in)
    groups = NB // local_blocks
    pieces = 2 if local_blocks % 2 == 0 else 1
    part = local_blocks // pieces
    spans = [slice(n * part, (n + 1) * part) for n in range(pieces)]
    wones = [fetch(first_factor[s]) for s in spans]
    wfour = fetch(fourth_factor)
    wtwo = fetch(second_factor)
    wthree = fetch(third_factor)
    received = []
    for s, w in zip(spans, wones):
        out = jnp.einsum("tbi,bij->bjt", inputs[:, s], w, preferred_element_type=F32).astype(BF16)
        received.append(send(split_units(out)))
    dw = jnp.einsum("tbo,bpo->bpt", grad_out, wfour, preferred_element_type=F32).astype(BF16)
    dw, received[-1] = follow(split_units(dw), received[-1])
    ddown_raw = send(dw)
    mixed = join_halves(received, groups)
    pre = jnp.einsum("cpt,cpm->cmt", mixed, wtwo, preferred_element_type=F32)
    act, slope = gelu_both(pre)
    hidden = act.astype(BF16)
    down = jnp.einsum("cmt,cmn->cnt", hidden, wthree, preferred_element_type=F32).astype(BF16)
    down, ddown_raw = follow(split_units(down), ddown_raw)
    regrouped_raw = send(down)
    ddown = join_halves([ddown_raw], groups)
    dhidden = jnp.einsum("cnt,cmn->cmt", ddown, wthree, preferred_element_type=F32)
    dpre = (dhidden * slope).astype(BF16)
    dz = jnp.einsum("cmt,cpm->cpt", dpre, wtwo, preferred_element_type=F32).astype(BF16)
    third_grad = jnp.einsum("cmt,cnt->cmn", hidden, ddown, preferred_element_type=F32)
    second_grad = jnp.einsum("cpt,cmt->cpm", mixed, dpre, preferred_element_type=F32)
    by_half = dz.reshape(local_blocks, groups, pieces, part * (HB // NB), tok)
    outs = [
        by_half[:, :, n]
        .reshape(local_blocks, groups * part, HB // NB, tok)
        .transpose(1, 0, 2, 3)
        for n in range(pieces)
    ]
    (outs, regrouped_raw) = follow(outs, regrouped_raw)
    in_parts, first_parts = [], []
    for n, (s, w) in enumerate(zip(spans, wones)):
        dy = join_halves([send(outs[n])], groups)
        grad = jnp.einsum("tbi,bjt->bij", inputs[:, s], dy, preferred_element_type=F32)
        first_parts.append(grad.astype(BF16))
        in_parts.append(
            jnp.einsum("bjt,bij->tbi", dy, w, preferred_element_type=F32)
            .astype(BF16)
            .reshape(tok, part * block_in)
        )
    regrouped = join_halves([regrouped_raw], groups)
    result = jnp.einsum("bpt,bpo->tbo", regrouped, wfour, preferred_element_type=F32).astype(BF16)
    result = result.reshape(tok, local_blocks * block_in)
    fourth_grad = jnp.einsum("bpt,tbo->bpo", regrouped, grad_out, preferred_element_type=F32)
    return (
        result,
        jnp.concatenate(in_parts, axis=1),
        scatter(jnp.concatenate(first_parts, axis=0)),
        scatter(second_grad),
        scatter(third_grad),
        scatter(fourth_grad),
    )


def solution(mesh):
    in_specs = (
        P("fsdp", "tensor"),
        P("tensor", "fsdp", None),
        P("tensor", "fsdp", None),
        P("tensor", "fsdp", None),
        P("tensor", "fsdp", None),
        P("fsdp", "tensor"),
    )
    out_specs = (
        P("fsdp", "tensor"),
        P("fsdp", "tensor"),
        P("tensor", "fsdp", None),
        P("tensor", "fsdp", None),
        P("tensor", "fsdp", None),
        P("tensor", "fsdp", None),
    )
    return jax.shard_map(local, mesh=mesh, in_specs=in_specs, out_specs=out_specs, check_vma=False)
```

```python
import jax
import jax.numpy as jnp
from jax import lax
from jax.sharding import PartitionSpec as P

D = 8192
NB = 64
HB = 512
F32 = jnp.float32
BF16 = jnp.bfloat16


def gelu_both(v):
    half = 0.5 * (1.0 + lax.erf(v * 0.7071067811865476))
    slope = half + v * jnp.exp(-0.5 * v * v) * 0.3989422804014327
    return v * half, slope


LINES = 4
CHUNKS = 2


def follow(value, done):
    return lax.optimization_barrier((value, done))


def line_groups(cols):
    return [[z * cols + x for z in range(LINES)] for x in range(cols)]


def col_groups(cols):
    return [[z * cols + x for x in range(cols)] for z in range(LINES)]


def line_step(arr, cols, hop, reach):
    if hop > 0:
        lines = range(reach - 1, LINES - 1)
        pairs = [(z * cols + x, (z + 1) * cols + x) for z in lines for x in range(cols)]
    else:
        lines = range(1, LINES - reach + 1)
        pairs = [(z * cols + x, (z - 1) * cols + x) for z in lines for x in range(cols)]
    return lax.ppermute(arr, "tensor", pairs)


def line_gather(own, cols, line):
    ups, downs = [own], [own]
    for reach in range(1, LINES):
        ups.append(line_step(ups[-1], cols, 1, reach))
        downs.append(line_step(downs[-1], cols, -1, reach))
    slots = [own]
    for r in range(1, LINES):
        slots.append(jnp.where(line >= r, ups[r], downs[LINES - r]))
    return slots, ups[1]


def line_pairs(cols, hop, far):
    if hop > 0:
        lines = range(0, LINES - far)
    else:
        lines = range(far, LINES)
    return [(z * cols + x, (z + hop) * cols + x) for z in lines for x in range(cols)]


def line_scatter(parts, cols):
    up = down = None
    for far in range(LINES - 1, 0, -1):
        u, d = parts[LINES - far], parts[far]
        if up is not None:
            u, d = u + up, d + down
        up = lax.ppermute(u, "tensor", line_pairs(cols, 1, far))
        down = lax.ppermute(d, "tensor", line_pairs(cols, -1, far))
        if far == 2:
            mark = up
    return parts[0] + (up + down), mark


def turn(arr, line):
    flipped = arr[::-1]
    twice = jnp.concatenate([flipped, flipped], axis=0)
    return lax.dynamic_slice_in_dim(twice, LINES - 1 - line, LINES, axis=0)


def to_col(units, cols, own):
    tok = units.shape[3]
    parts = units.reshape(LINES, own, cols, own, HB // NB, tok).transpose(2, 0, 1, 3, 4, 5)
    got = lax.all_to_all(
        parts, "tensor", 0, 0, axis_index_groups=col_groups(cols), tiled=True
    )
    return got.transpose(3, 1, 0, 2, 4, 5).reshape(own, HB, tok)


def from_col(units, cols, own):
    tok = units.shape[2]
    parts = units.reshape(own, LINES, cols, own, HB // NB, tok).transpose(2, 1, 3, 0, 4, 5)
    got = lax.all_to_all(
        parts, "tensor", 0, 0, axis_index_groups=col_groups(cols), tiled=True
    )
    return got.transpose(1, 2, 0, 3, 4, 5).reshape(LINES, own, HB // LINES, tok)


def line_swap(arr, cols):
    return lax.all_to_all(arr, "tensor", 0, 0, axis_index_groups=line_groups(cols), tiled=True)


def scatter(grad, axis):
    return lax.psum_scatter(grad, "fsdp", scatter_dimension=axis, tiled=True)


def local(activations, first_factor, second_factor, third_factor, fourth_factor, out_grad):
    tok = activations.shape[0]
    own = second_factor.shape[0]
    block_in = D // NB
    cols = NB // own // LINES
    wide = HB // LINES
    line = lax.axis_index("tensor") // cols
    step = tok // CHUNKS

    rows = first_factor.shape[1]
    wone = first_factor.reshape(own, rows, LINES, wide).transpose(2, 0, 1, 3)
    wone = turn(line_swap(wone, cols), line)
    wone = lax.all_gather(wone, "fsdp", axis=2, tiled=True)

    gathered = []
    last = None
    for n in range(CHUNKS):
        for arr in (activations, out_grad):
            shard = arr[n * step : (n + 1) * step]
            if last is not None:
                shard, gate = follow(shard, last[1])
            slots, mark = line_gather(shard, cols, line)
            last = (slots, mark)
            gathered.append([v.reshape(step, own, block_in) for v in slots])

    wfour = lax.all_gather(fourth_factor, "fsdp", axis=1, tiled=True)
    wfour = wfour.reshape(own, LINES, wide, block_in).transpose(1, 0, 2, 3)
    wfour = turn(line_swap(wfour, cols), line)
    wtwo = lax.all_gather(second_factor, "fsdp", axis=1, tiled=True)
    wthree = lax.all_gather(third_factor, "fsdp", axis=1, tiled=True)
    wtwo = turn(
        wtwo.reshape(own, LINES, wide, HB).transpose(1, 0, 2, 3), line
    ).transpose(1, 0, 2, 3).reshape(own, HB, HB)
    wthree = turn(
        wthree.reshape(own, HB, LINES, wide).transpose(2, 0, 1, 3), line
    ).transpose(1, 2, 0, 3).reshape(own, HB, HB)

    results, in_grads = [], []
    sums = [0.0, 0.0, 0.0, 0.0]
    for n in range(CHUNKS):
        xg = jnp.stack(gathered[2 * n])
        gg = jnp.stack(gathered[2 * n + 1])
        out = jnp.einsum("ztbi,zbij->zbjt", xg, wone, preferred_element_type=F32).astype(BF16)
        if n:
            out, regrouped = follow(out, regrouped)
        mixed = to_col(out, cols, own)
        dw = jnp.einsum("ztbo,zbpo->zbpt", gg, wfour, preferred_element_type=F32).astype(BF16)
        ddown = to_col(dw, cols, own)
        pre = jnp.einsum("cpt,cpm->cmt", mixed, wtwo, preferred_element_type=F32)
        act, slope = gelu_both(pre)
        hidden = act.astype(BF16)
        down = jnp.einsum("cmt,cmn->cnt", hidden, wthree, preferred_element_type=F32)
        down = down.astype(BF16)
        if n:
            down, results[-1][1] = follow(down, results[-1][1])
        regrouped = from_col(down, cols, own)
        dhidden = jnp.einsum("cnt,cmn->cmt", ddown, wthree, preferred_element_type=F32)
        dpre = (dhidden * slope).astype(BF16)
        dz = jnp.einsum("cmt,cpm->cpt", dpre, wtwo, preferred_element_type=F32).astype(BF16)
        if n:
            dz, in_grads[-1][1] = follow(dz, in_grads[-1][1])
        dy = from_col(dz, cols, own)
        res = jnp.einsum("zbpt,zbpo->ztbo", regrouped, wfour, preferred_element_type=F32)
        res = res.astype(BF16).reshape(LINES, step, own * block_in)
        results.append(list(line_scatter([res[r] for r in range(LINES)], cols)))
        ing = jnp.einsum("zbjt,zbij->ztbi", dy, wone, preferred_element_type=F32)
        ing = ing.astype(BF16).reshape(LINES, step, own * block_in)
        in_grads.append(list(line_scatter([ing[r] for r in range(LINES)], cols)))
        terms = (
            jnp.einsum("ztbi,zbjt->zbij", xg, dy, preferred_element_type=F32),
            jnp.einsum("cpt,cmt->cpm", mixed, dpre, preferred_element_type=F32),
            jnp.einsum("cmt,cnt->cmn", hidden, ddown, preferred_element_type=F32),
            jnp.einsum("zbpt,ztbo->zbpo", regrouped, gg, preferred_element_type=F32),
        )
        sums = [a + b for a, b in zip(sums, terms)]
    first_grad = scatter(turn(sums[0].astype(BF16), line), 2)
    first_grad = line_swap(first_grad, cols).transpose(1, 2, 0, 3).reshape(own, rows, HB)
    second_grad = turn(
        sums[1].astype(BF16).reshape(own, LINES, wide, HB).transpose(1, 0, 2, 3), line
    ).transpose(1, 0, 2, 3).reshape(own, HB, HB)
    third_grad = turn(
        sums[2].astype(BF16).reshape(own, HB, LINES, wide).transpose(2, 0, 1, 3), line
    ).transpose(1, 2, 0, 3).reshape(own, HB, HB)
    fourth_grad = line_swap(turn(sums[3].astype(BF16), line), cols)
    fourth_grad = fourth_grad.transpose(1, 0, 2, 3).reshape(own, HB, block_in)
    return (
        jnp.concatenate([r[0] for r in results], axis=0),
        jnp.concatenate([r[0] for r in in_grads], axis=0),
        first_grad.astype(F32),
        scatter(second_grad, 1).astype(F32),
        scatter(third_grad, 1).astype(F32),
        scatter(fourth_grad, 1).astype(F32),
    )


def solution(mesh):
    in_specs = (
        P("fsdp", "tensor"),
        P("tensor", "fsdp", None),
        P("tensor", "fsdp", None),
        P("tensor", "fsdp", None),
        P("tensor", "fsdp", None),
        P("fsdp", "tensor"),
    )
    out_specs = (
        P("fsdp", "tensor"),
        P("fsdp", "tensor"),
        P("tensor", "fsdp", None),
        P("tensor", "fsdp", None),
        P("tensor", "fsdp", None),
        P("tensor", "fsdp", None),
    )
    return jax.shard_map(local, mesh=mesh, in_specs=in_specs, out_specs=out_specs, check_vma=False)
```
